256 devices in a mesh: ens: 16 (over z, y_hi), mp: 16 (over x, y_lo, core).
Axes of the slice: x: 4, y: 4 (y_hi: 2, y_lo: 2; y = y_hi * 2 + y_lo), z: 8, core: 2. Of those that a mesh axis runs over, the one named last changes fastest.
Arguments:
- tokens: bfloat16 [16, 8192, 1024], P('ens', 'mp'), may hold values from -6 to 6
- ln_gain: float32 [1024], replicated, may hold values from 0.5 to 1.5
- w_qkv: bfloat16 [1024, 3072], replicated, may hold values from -1 to 1
- w_out: bfloat16 [1024, 1024], replicated, may hold values from -0.75 to 0.75
- neighbours: int32 [4, 32768], P(None, 'mp'), may hold values from 0 to 8191, as said below
- edge_weights: float32 [4, 32768], P(None, 'mp'), may hold values from 0.2 to 1
- w_dec: bfloat16 [100, 1024], replicated, may hold values from -0.1875 to 0.1875
- truth: float32 [100, 32768], P(None, ('mp', 'ens')), may hold values from -6 to 6
Outputs:
- crps_score: float32 [100, 32768], P(None, ('mp', 'ens'))
The draws below stay inside these ranges and needn't reach their ends.
Inputs may be any that keep to these rules, and one draw needn't show every extreme that they name: `neighbours`: the tokens of point g are among tokens g // 2048 * 512 to g // 2048 * 512 + 511 of its member.
All inputs are finite; a program needn't handle non-finite values.
Results may differ from the reference program's by a relative error of at most 0.0028.
The reference program's roundings to bfloat16 on the way (of `normed`, `projected`, `weights`, `context`, `processed`, `hidden` and `decoded`) count: a program that leaves them out, or rounds other values in their place, can miss the bound.
Values may be sent and summed in bfloat16 or wider, within the bound.
A program may use at most 128 MiB of HBM per device.

```python
import jax
import jax.numpy as jnp
from jax import lax

D = 1024
HEADS = 16
VARS = 100
NEIGH = 4
HALF = 512
TOK_DEV = 512
GP_DEV = 2048
MEMBERS = 16
TOKENS = 8192
GRID = 32768
N_MP = 16


def draw_w_qkv(key, part):
    base = jax.random.normal(key, (D, 3 * D), jnp.float32) * D ** (-0.5)
    return jnp.clip(base, -1.0, 1.0).astype(jnp.bfloat16)


def draw_neighbours(key, part):
    block_first = jnp.arange(GRID, dtype=jnp.int32) // GP_DEV * TOK_DEV
    offsets = jax.random.randint(key, (NEIGH, GRID), 0, TOK_DEV, dtype=jnp.int32)
    result = block_first[None, :] + offsets
    result = result.at[0, 0].set(0)
    result = result.at[0, GRID - 1].set(TOKENS - 1)
    return result.astype(jnp.int32)


def level_of(rng, shape, pieces, least, top_value):
    gain = 1.0
    for dim, shards_of in pieces:
        draws = jax.random.uniform(jax.random.fold_in(jax.random.fold_in(rng, 6), dim), (shards_of,), jnp.float32, least / len(pieces), top_value / len(pieces))
        gain = gain * jnp.repeat(jnp.exp(draws), shape[dim] // shards_of).reshape((-1,) + (1,) * (len(shape) - 1 - dim))
    return gain


def gaussian(own_key, extent, width, reach, shards=(), held_as=jnp.bfloat16):
    factor_of = level_of(own_key, extent, shards, -0.22, 0.18) if shards else 1.0
    entries = jax.random.normal(own_key, extent, jnp.float32) * width * factor_of
    return jnp.minimum(jnp.maximum(entries, -reach), reach).astype(held_as)


def setup_inputs(seed: int = 0) -> dict:
    key_of = jax.random.split(jax.random.key(seed), 9)
    return {
        "tokens": gaussian(key_of[0], (MEMBERS, TOKENS, D), 1.0, 6.0, ((0, 16), (1, 16))),
        "ln_gain": jnp.clip(1.0 + 0.1 * jax.random.normal(key_of[1], (D,), jnp.float32), 0.5, 1.5),
        "w_qkv": draw_w_qkv(jax.random.fold_in(key_of[8], 71), 0),
        "w_out": gaussian(key_of[3], (D, D), (D // 16) ** -0.5, 0.75),
        "neighbours": draw_neighbours(jax.random.fold_in(key_of[8], 71), 0),
        "edge_weights": jnp.clip(0.2 + 0.8 * jax.random.uniform(key_of[5], (NEIGH, GRID), jnp.float32) ** level_of(key_of[5], (NEIGH, GRID), ((1, 16),), -0.2, 0.2), 0.2, 1.0),
        "w_dec": gaussian(key_of[6], (VARS, D), D ** -0.5, 0.1875),
        "truth": gaussian(key_of[7], (VARS, GRID), 1.0, 6.0, ((1, 256),), jnp.float32),
    }


ALPHA = 0.95

def layer_norm(inputs, ln_gain):
    values = inputs.astype(jnp.float32)
    average = lax.optimization_barrier(jnp.mean(values, axis=-1, keepdims=True))
    centred = values - average
    variance = lax.optimization_barrier(jnp.mean(centred * centred, axis=-1, keepdims=True))
    return (centred * lax.rsqrt(variance + 1e-05) * ln_gain).astype(jnp.bfloat16)

def attend(queries, key_rows, value_rows, first_row, seq_tokens):
    count = queries.shape[0]
    head_dim = queries.shape[-1]
    scores = jnp.einsum('qhe,khe->hqk', queries.astype(jnp.float32), key_rows.astype(jnp.float32)) / jnp.sqrt(jnp.float32(head_dim))
    query_pos = first_row + jnp.arange(count)
    key_pos = first_row - HALF + jnp.arange(count + 2 * HALF)
    allowed = (key_pos[None, :] >= 0) & (key_pos[None, :] < seq_tokens) & (jnp.abs(key_pos[None, :] - query_pos[:, None]) <= HALF)
    scores = jnp.where(allowed[None], scores, -1e+30)
    top = lax.optimization_barrier(jnp.max(scores, axis=-1, keepdims=True))
    expo = jnp.exp(scores - top)
    weights = (expo / lax.optimization_barrier(jnp.sum(expo, axis=-1, keepdims=True))).astype(jnp.bfloat16)
    context = jnp.einsum('hqk,khe->qhe', weights.astype(jnp.float32), value_rows.astype(jnp.float32))
    return context.astype(jnp.bfloat16)

def reference(tokens, ln_gain, w_qkv, w_out, neighbours, edge_weights, w_dec, truth):
    head_dim = D // HEADS

    def one_member(member_tokens):
        normed = layer_norm(member_tokens, ln_gain)
        projected = jnp.dot(normed, w_qkv, preferred_element_type=jnp.float32).astype(jnp.bfloat16)
        queries = projected[:, :D].reshape(TOKENS, HEADS, head_dim)
        key_rows = projected[:, D:2 * D].reshape(TOKENS, HEADS, head_dim)
        value_rows = projected[:, 2 * D:].reshape(TOKENS, HEADS, head_dim)
        key_pad = jnp.pad(key_rows, ((HALF, HALF), (0, 0), (0, 0)))
        value_pad = jnp.pad(value_rows, ((HALF, HALF), (0, 0), (0, 0)))

        def block_attend(block_index):
            first_row = block_index * TOK_DEV
            query_block = lax.dynamic_slice_in_dim(queries, first_row, TOK_DEV, 0)
            key_block = lax.dynamic_slice_in_dim(key_pad, first_row, TOK_DEV + 2 * HALF, 0)
            value_block = lax.dynamic_slice_in_dim(value_pad, first_row, TOK_DEV + 2 * HALF, 0)
            return attend(query_block, key_block, value_block, first_row, TOKENS)
        context = lax.map(block_attend, jnp.arange(N_MP, dtype=jnp.int32)).reshape(TOKENS, D)
        proj_out = jnp.dot(context, w_out, preferred_element_type=jnp.float32)
        processed = (member_tokens.astype(jnp.float32) + proj_out).astype(jnp.bfloat16)
        hidden = jnp.zeros((GRID, D), jnp.float32)
        for slot_index in range(NEIGH):
            picked = jnp.take(processed, neighbours[slot_index], axis=0)
            hidden = hidden + edge_weights[slot_index][:, None] * picked.astype(jnp.float32)
        decoded = jnp.dot(w_dec, hidden.astype(jnp.bfloat16).T, preferred_element_type=jnp.float32)
        return decoded.astype(jnp.bfloat16)
    decoded = lax.map(one_member, tokens).astype(jnp.float32)
    skill_term = lax.optimization_barrier(jnp.mean(jnp.abs(decoded - truth[None]), axis=0))
    spread = jnp.zeros_like(truth)
    for member_index in range(MEMBERS):
        spread = spread + lax.optimization_barrier(jnp.sum(jnp.abs(decoded[member_index][None] - decoded), axis=0))
    coeff = ALPHA / (2.0 * MEMBERS * (MEMBERS - 1)) + (1.0 - ALPHA) / (2.0 * MEMBERS * MEMBERS)
    return skill_term - coeff * spread
```

```python
import functools

import jax
import jax.numpy as jnp
from jax import lax
from jax.experimental import pallas as pl
from jax.experimental.pallas import tpu as pltpu
from jax.sharding import PartitionSpec as P

HEADS = 16
NEIGH = 4
HALF = 512
ALPHA = 0.95
F32 = jnp.float32
BF16 = jnp.bfloat16
MESH = pl.DeviceIdType.MESH


def dot(a, b):
    return lax.dot_general(a, b, (((1,), (0,)), ((), ())), preferred_element_type=F32)


def dot_t(a, b):
    return lax.dot_general(a, b, (((1,), (1,)), ((), ())), preferred_element_type=F32)


def split(x):
    hi = x.astype(BF16)
    lo = (x - hi.astype(F32)).astype(BF16)
    return hi, lo


def norm_rows(src, dst, gain_ref, rows):
    block = 64

    def step(i, carry):
        sl = pl.ds(pl.multiple_of(i * block, block), block)
        x = src[sl, :].astype(F32)
        mean = jnp.mean(x, axis=-1, keepdims=True)
        c = x - mean
        var = jnp.mean(c * c, axis=-1, keepdims=True)
        dst[sl, :] = (c * lax.rsqrt(var + 1e-05) * gain_ref[...]).astype(BF16)
        return carry

    lax.fori_loop(0, rows // block, step, 0)


def kernel(
    n_ens, n_mp, rows, grid_rows, n_vars,
    tok_hbm, gain_ref, wqkv_hbm, wout_hbm, nbr_ref, ew_ref, wdec_ref, truth_ref,
    out_ref,
    tok, halo, wqkv, wout, normed, qkv, kv, bias, o_acc, m_acc, l_acc, ctx, w2, sel_hi, sel_lo,
    d_hl, dec, got,
    in_sem, send_sem, recv_sem, a2a_send, a2a_recv,
):
    width = tok.shape[1]
    pairs = width // 128
    me = lax.axis_index("mp")
    ens = lax.axis_index("ens")
    core = lax.rem(me, 2)
    partner = me + 1 - 2 * core
    other = me - 1 + 2 * core
    has_other = jnp.logical_and(other >= 0, other < n_mp)

    loads = [
        pltpu.make_async_copy(tok_hbm.at[0], tok, in_sem.at[0]),
        pltpu.make_async_copy(wqkv_hbm, wqkv, in_sem.at[1]),
        pltpu.make_async_copy(wout_hbm, wout, in_sem.at[2]),
    ]
    for load in loads:
        load.start()

    barrier = pltpu.get_barrier_semaphore()
    pl.semaphore_signal(barrier, inc=1, device_id={"mp": partner}, device_id_type=MESH)

    around = lax.rem(other + n_mp, n_mp)
    pl.semaphore_signal(barrier, inc=1, device_id={"mp": around}, device_id_type=MESH)
    for step in range(1, n_ens):
        peer = lax.rem(ens + step, n_ens)
        pl.semaphore_signal(barrier, inc=1, device_id={"ens": peer}, device_id_type=MESH)

    loads[0].wait()
    norm_rows(tok, normed, gain_ref, rows)

    pl.semaphore_wait(barrier, n_ens + 1)

    def send_to(slot, target):
        return pltpu.make_async_remote_copy(
            src_ref=tok_hbm.at[0],
            dst_ref=halo.at[slot],
            send_sem=send_sem.at[slot],
            recv_sem=recv_sem.at[slot],
            device_id={"mp": target},
            device_id_type=MESH,
        )

    send_to(0, partner).start()

    @pl.when(has_other)
    def _():
        send_to(1, other).start()

    loads[1].wait()
    chunk = 512
    n_q = width // chunk

    def project_q(i, carry):
        cols = pl.ds(pl.multiple_of(i * chunk, chunk), chunk)
        qkv[:, cols] = dot(normed[...], wqkv[:, cols]).astype(BF16) * 0.125
        return carry

    def project_kv(i, carry):
        cols = pl.ds(pl.multiple_of(width + i * chunk, chunk), chunk)
        qkv[:, cols] = dot(normed[...], wqkv[:, cols]).astype(BF16)
        return carry

    lax.fori_loop(0, n_q, project_q, 0)
    lax.fori_loop(0, 2 * n_q, project_kv, 0)

    ones = jnp.ones((rows, 128), BF16)
    half_rows = rows // 2
    ones_h = jnp.ones((half_rows, 128), BF16)

    def first_half(n):
        return lax.broadcasted_iota(jnp.int32, (n, 128), 1) < 64

    def own_pair(hp, carry):
        cols = pl.ds(pl.multiple_of(hp * 128, 128), 128)
        kcols = pl.ds(pl.multiple_of(width + hp * 128, 128), 128)
        vcols = pl.ds(pl.multiple_of(2 * width + hp * 128, 128), 128)
        k = qkv[:, kcols]
        vx = jnp.concatenate([qkv[:, vcols], ones], axis=1)
        lanes = first_half(half_rows)
        for t in range(2):
            rs = pl.ds(t * half_rows, half_rows)
            q = qkv[rs, cols]
            zero = jnp.zeros_like(q)
            parts = []
            for part in range(2):
                qm = jnp.where(lanes, q, zero) if part == 0 else jnp.where(lanes, zero, q)
                s = dot_t(qm, k)
                m = jnp.max(s, axis=1, keepdims=True)
                p = jnp.exp(s - m).astype(BF16)
                parts.append((dot(p, vx), m))
            (o0, m0), (o1, m1) = parts
            o_acc[rs, cols] = jnp.where(lanes, o0[:, :128], o1[:, :128])
            l_acc[rs, cols] = jnp.where(lanes, o0[:, 128:], o1[:, 128:])
            m_acc[rs, cols] = jnp.where(lanes, m0, m1)
        return carry

    lax.fori_loop(0, pairs, own_pair, 0)

    loads[2].wait()
    w2_hi, w2_lo = split(dot_t(wdec_ref[...], wout[...]))
    w2[0] = w2_hi
    w2[1] = w2_lo
    base = me * rows
    gchunk = 256

    def build(i, carry):
        cols = pl.ds(pl.multiple_of(i * gchunk, gchunk), gchunk)
        t = lax.broadcasted_iota(jnp.int32, (rows, gchunk), 0)
        acc = jnp.zeros((rows, gchunk), F32)
        for k in range(NEIGH):
            idx = nbr_ref[k : k + 1, cols] - base
            w = ew_ref[k : k + 1, cols]
            acc = acc + jnp.where(t == idx, w, 0.0)
        hi, lo = split(acc)
        sel_hi[:, cols] = hi
        sel_lo[:, cols] = lo
        return carry

    lax.fori_loop(0, grid_rows // gchunk, build, 0)

    def segment(slot, left):
        norm_rows(halo.at[slot], normed, gain_ref, rows)

        def project(i, carry):
            src = pl.ds(pl.multiple_of(width + i * chunk, chunk), chunk)
            dst = pl.ds(pl.multiple_of(i * chunk, chunk), chunk)
            kv[:, dst] = dot(normed[...], wqkv[:, src]).astype(BF16)
            return carry

        lax.fori_loop(0, 2 * n_q, project, 0)
        sign = 2 * left - 1
        ii = lax.broadcasted_iota(jnp.int32, (half_rows, half_rows), 0)
        jj = lax.broadcasted_iota(jnp.int32, (half_rows, half_rows), 1)
        bias[...] = jnp.where((jj - ii) * sign >= 0, 0.0, -1e30)
        near = pl.multiple_of((1 - left) * half_rows, half_rows)
        far = pl.multiple_of(left * half_rows, half_rows)

        def pair(hp, carry):
            cols = pl.ds(pl.multiple_of(hp * 128, 128), 128)
            vcols = pl.ds(pl.multiple_of(width + hp * 128, 128), 128)
            lanes = first_half(half_rows)
            k_n = kv[pl.ds(near, half_rows), cols]
            k_f = kv[pl.ds(far, half_rows), cols]
            v_n = jnp.concatenate([kv[pl.ds(near, half_rows), vcols], ones_h], axis=1)
            v_f = jnp.concatenate([kv[pl.ds(far, half_rows), vcols], ones_h], axis=1)
            for wide in (True, False):
                rs = pl.ds(near if wide else far, half_rows)
                q = qkv[rs, cols]
                zero = jnp.zeros_like(q)
                parts = []
                for part in range(2):
                    qm = jnp.where(lanes, q, zero) if part == 0 else jnp.where(lanes, zero, q)
                    if wide:
                        s_n = dot_t(qm, k_n) + bias[...]
                        s_f = dot_t(qm, k_f)
                        m = jnp.maximum(
                            jnp.max(s_n, axis=1, keepdims=True), jnp.max(s_f, axis=1, keepdims=True)
                        )
                        o = dot(jnp.exp(s_n - m).astype(BF16), v_n)
                        o = o + dot(jnp.exp(s_f - m).astype(BF16), v_f)
                    else:
                        s_f = dot_t(qm, k_f) + bias[...]
                        m = jnp.max(s_f, axis=1, keepdims=True)
                        o = dot(jnp.exp(s_f - m).astype(BF16), v_f)
                    parts.append((o, m))
                (o0, m0), (o1, m1) = parts
                o = jnp.where(lanes, o0[:, :128], o1[:, :128])
                l = jnp.where(lanes, o0[:, 128:], o1[:, 128:])
                m = jnp.where(lanes, m0, m1)
                m_old = m_acc[rs, cols]
                m_new = jnp.maximum(m_old, m)
                a = jnp.exp(m_old - m_new)
                b = jnp.exp(m - m_new)
                o_acc[rs, cols] = o_acc[rs, cols] * a + o * b
                l_acc[rs, cols] = l_acc[rs, cols] * a + l * b
                m_acc[rs, cols] = m_new
            return carry

        lax.fori_loop(0, pairs, pair, 0)

    send_to(0, partner).wait()
    segment(0, core)

    @pl.when(has_other)
    def _():
        send_to(1, other).wait()
        segment(1, 1 - core)

    def finish(i, carry):
        sl = pl.ds(pl.multiple_of(i * 32, 32), 32)
        ctx[sl, :] = (o_acc[sl, :] / l_acc[sl, :]).astype(BF16)
        return carry

    lax.fori_loop(0, rows // 32, finish, 0)

    d = dot_t(w2[0], ctx[...]) + dot_t(w2[1], ctx[...]) + dot_t(wdec_ref[...], tok[...])
    d_hi, d_lo = split(d)
    d_hl[0] = d_hi
    d_hl[1] = d_lo
    points = grid_rows // n_ens
    per = gchunk // points

    def decode(i, carry):
        cols = pl.ds(pl.multiple_of(i * gchunk, gchunk), gchunk)
        hi = sel_hi[:, cols]
        r = dot(d_hl[0], hi) + dot(d_hl[1], hi) + dot(d_hl[0], sel_lo[:, cols])
        r = r.astype(BF16)
        for j in range(per):
            dec[i * per + j] = r[:, j * points : (j + 1) * points]
        return carry

    lax.fori_loop(0, grid_rows // gchunk, decode, 0)

    def to_peer(step):
        peer = lax.rem(ens + step, n_ens)
        return pltpu.make_async_remote_copy(
            src_ref=dec.at[peer],
            dst_ref=got.at[step],
            send_sem=a2a_send.at[step],
            recv_sem=a2a_recv.at[step],
            device_id={"ens": peer},
            device_id_type=MESH,
        )

    for step in range(1, n_ens):
        to_peer(step).start()
    got[0] = dec[ens]
    for step in range(1, n_ens):
        to_peer(step).wait()

    coeff = ALPHA / (2.0 * n_ens * (n_ens - 1)) + (1.0 - ALPHA) / (2.0 * n_ens * n_ens)

    def score(sl):
        truth = truth_ref[sl, :]
        members = [got[j, sl, :].astype(F32) for j in range(n_ens)]
        skill = jnp.zeros_like(truth)
        spread = jnp.zeros_like(truth)
        for j in range(n_ens):
            skill = skill + jnp.abs(members[j] - truth)
            for k in range(j + 1, n_ens):
                spread = spread + jnp.abs(members[j] - members[k])
        out_ref[sl, :] = skill * (1.0 / n_ens) - (2.0 * coeff) * spread

    def score_block(i, carry):
        score(pl.ds(pl.multiple_of(i * 16, 16), 16))
        return carry

    whole = n_vars // 16
    lax.fori_loop(0, whole, score_block, 0)
    if n_vars % 16:
        score(slice(whole * 16, n_vars))


def solution(mesh):
    n_ens, n_mp = mesh.shape["ens"], mesh.shape["mp"]

    def shards(tokens, ln_gain, w_qkv, w_out, neighbours, edge_weights, w_dec, truth):
        rows, width = tokens.shape[1:]
        grid_rows = neighbours.shape[1]
        n_vars, points = truth.shape
        hbm = pl.BlockSpec(memory_space=pl.ANY)
        vmem = pl.BlockSpec(memory_space=pltpu.VMEM)
        return pl.pallas_call(
            functools.partial(kernel, n_ens, n_mp, rows, grid_rows, n_vars),
            out_shape=jax.ShapeDtypeStruct((n_vars, points), F32),
            in_specs=[hbm, vmem, hbm, hbm, vmem, vmem, vmem, vmem],
            out_specs=vmem,
            scratch_shapes=[
                pltpu.VMEM((rows, width), BF16),
                pltpu.VMEM((2, rows, width), BF16),
                pltpu.VMEM((width, 3 * width), BF16),
                pltpu.VMEM((width, width), BF16),
                pltpu.VMEM((rows, width), BF16),
                pltpu.VMEM((rows, 3 * width), BF16),
                pltpu.VMEM((rows, 2 * width), BF16),
                pltpu.VMEM((rows // 2, rows // 2), F32),
                pltpu.VMEM((rows, width), F32),
                pltpu.VMEM((rows, width), F32),
                pltpu.VMEM((rows, width), F32),
                pltpu.VMEM((rows, width), BF16),
                pltpu.VMEM((2, n_vars, width), BF16),
                pltpu.VMEM((rows, grid_rows), BF16),
                pltpu.VMEM((rows, grid_rows), BF16),
                pltpu.VMEM((2, n_vars, rows), BF16),
                pltpu.VMEM((n_ens, n_vars, points), BF16),
                pltpu.VMEM((n_ens, n_vars, points), BF16),
                pltpu.SemaphoreType.DMA((3,)),
                pltpu.SemaphoreType.DMA((2,)),
                pltpu.SemaphoreType.DMA((2,)),
                pltpu.SemaphoreType.DMA((n_ens,)),
                pltpu.SemaphoreType.DMA((n_ens,)),
            ],
            compiler_params=pltpu.CompilerParams(
                collective_id=0, has_side_effects=True, vmem_limit_bytes=62 * 1024 * 1024
            ),
        )(tokens, ln_gain.reshape(1, width), w_qkv, w_out, neighbours, edge_weights, w_dec, truth)

    in_specs = (
        P("ens", "mp", None),
        P(),
        P(),
        P(),
        P(None, "mp"),
        P(None, "mp"),
        P(),
        P(None, ("mp", "ens")),
    )
    out_specs = P(None, ("mp", "ens"))
    return jax.shard_map(shards, mesh=mesh, in_specs=in_specs, out_specs=out_specs, check_vma=False)
```
